32 devices in a mesh: groups: 1, seq: 32 (over z, y, x, core), tensor: 1.
Axes of the slice: x: 2, y: 2, z: 4, core: 2. Of those that a mesh axis runs over, the one named last changes fastest.
Arguments:
- queries: bfloat16 [256, 2048], P(('groups', 'seq'), 'tensor'), may hold values from -15.75 to 15.75
- span_keys: bfloat16 [256, 1024], P(('groups', 'seq'), 'tensor'), may hold values from -6 to 6
- span_values: bfloat16 [256, 1024], P(('groups', 'seq'), 'tensor'), may hold values from -6 to 6
- cache_keys: bfloat16 [4096, 1024], P(('groups', 'seq'), 'tensor'), may hold values from -10.4 to 10.4
- cache_values: bfloat16 [4096, 1024], P(('groups', 'seq'), 'tensor'), may hold values from -6 to 6
- cache_valid: int32 [4096], P(('groups', 'seq')), may hold values 0 or 1
- span_start: int32 [1], P('groups'), may hold values from 2048 to 4096
Outputs:
- attended: bfloat16 [256, 2048], P(('groups', 'seq'), 'tensor')
The draws below stay inside these ranges and needn't reach their ends.
All inputs are finite; a program needn't handle non-finite values. No bound on the sum of `cache_valid` on one device may be relied on, other than what follows from the above.
Results may differ from the reference program's by a relative error of at most 0.01.
Values may be sent and summed in bfloat16 or wider, within the bound.
A program may use at most 64 MiB of HBM per device.

```python
import jax
import jax.numpy as jnp
from jax import lax

HEADS = 16
KV_HEADS = 8
HEAD_DIM = 128
SPAN_DEV = 8
CACHE_DEV = 128
SPAN = 256
CACHE = 4096
N_SEQ = 32


def cache_entries(key):
    base_key = jax.random.fold_in(key, 11)
    shape = (CACHE, KV_HEADS * HEAD_DIM)
    entries = jnp.clip(jax.random.normal(base_key, shape, jnp.float32), -6.0, 6.0)
    return entries


def draw_cache_keys(key, part):
    entries = cache_entries(key)
    return entries.astype(jnp.bfloat16)


def draw_queries(key, part):
    base_key = jax.random.fold_in(key, 23)
    shape = (SPAN, HEADS * HEAD_DIM)
    entries = jnp.clip(3.5 * jax.random.normal(base_key, shape, jnp.float32), -15.75, 15.75)
    return entries.astype(jnp.bfloat16)


def touch_ends(result, rng, low, top_value):
    index_at = [jax.random.randint(jax.random.fold_in(rng, axis), (), 0, length) for axis, length in enumerate(result.shape)]
    main_axis = result.shape.index(max(result.shape))
    next_to = index_at[:main_axis] + [(index_at[main_axis] + 1) % result.shape[main_axis]] + index_at[main_axis + 1:]
    return result.at[tuple(index_at)].set(low).at[tuple(next_to)].set(top_value)


def shard_levels(own_key, shape, split, smallest, top_value):
    loudness = 1.0
    for position, blocks in split:
        heights = jax.random.uniform(jax.random.fold_in(jax.random.fold_in(own_key, 6), position), (blocks,), jnp.float32, smallest / len(split), top_value / len(split))
        loudness = loudness * jnp.repeat(jnp.exp(heights), shape[position] // blocks).reshape((-1,) + (1,) * (len(shape) - 1 - position))
    return loudness


def scatter_about(rng, dims, width, bound, pieces=(), kind=jnp.bfloat16):
    gain = shard_levels(rng, dims, pieces, -0.22, 0.18) if pieces else 1.0
    array = jax.random.normal(rng, dims, jnp.float32) * width * gain
    return jnp.minimum(jnp.maximum(array, -bound), bound).astype(kind)


def setup_inputs(seed: int = 0, part: int = 0) -> dict:
    key_of = jax.random.split(jax.random.key(seed), 8)
    part_splits = jax.random.split(jax.random.fold_in(key_of[7], part), 8)
    return {
        "queries": draw_queries(jax.random.fold_in(jax.random.fold_in(key_of[7], part), 71), part),
        "span_keys": scatter_about(part_splits[1], (SPAN, KV_HEADS * HEAD_DIM), 1.0, 6.0, ((0, 32),)),
        "span_values": scatter_about(part_splits[2], (SPAN, KV_HEADS * HEAD_DIM), 1.0, 6.0, ((0, 32),)),
        "cache_keys": draw_cache_keys(jax.random.fold_in(jax.random.fold_in(key_of[7], part), 71), part),
        "cache_values": scatter_about(part_splits[4], (CACHE, KV_HEADS * HEAD_DIM), 1.0, 6.0, ((0, 32),)),
        "cache_valid": touch_ends((jax.random.randint(part_splits[5], (CACHE,), 0, 8) < 7).astype(jnp.int32), jax.random.fold_in(part_splits[5], 1), 0, 1),
        "span_start": jax.random.randint(part_splits[6], (1,), CACHE // 2, CACHE + 1).astype(jnp.int32),
    }


SCORE_SCALE = 168.0 ** -0.5
MASKED_SCORE = -1.0e30


def reference(queries, span_keys, span_values, cache_keys, cache_values, cache_valid, span_start):
    group_size = HEADS // KV_HEADS
    all_keys = jnp.concatenate([cache_keys, span_keys], axis=0)
    all_values = jnp.concatenate([cache_values, span_values], axis=0)
    slot_ids = jnp.arange(CACHE, dtype=jnp.int32)
    cache_live = (cache_valid == 1) & (slot_ids < span_start[0])
    span_ids = jnp.arange(SPAN, dtype=jnp.int32)
    span_live = span_ids[None, :] <= span_ids[:, None]
    visible = jnp.concatenate([jnp.broadcast_to(cache_live[None, :], (SPAN, CACHE)), span_live], axis=1)

    def one_head(head_index):
        kv_index = (head_index // group_size).astype(jnp.int32)
        query_head_rows = lax.dynamic_slice_in_dim(queries, (head_index * HEAD_DIM).astype(jnp.int32), HEAD_DIM, 1)
        key_head = lax.dynamic_slice_in_dim(all_keys, (kv_index * HEAD_DIM).astype(jnp.int32), HEAD_DIM, 1)
        value_head = lax.dynamic_slice_in_dim(all_values, (kv_index * HEAD_DIM).astype(jnp.int32), HEAD_DIM, 1)
        scores = jnp.dot(query_head_rows, key_head.T, preferred_element_type=jnp.float32) * SCORE_SCALE
        scores = jnp.where(visible, scores, MASKED_SCORE)
        peak = jnp.max(scores, axis=1, keepdims=True)
        expo = jnp.where(visible, jnp.exp(scores - peak), 0.0)
        weights = expo.astype(jnp.bfloat16).astype(jnp.float32)
        cache_score_weights = weights[:, :CACHE].reshape(SPAN, N_SEQ, CACHE_DEV)
        span_score_weights = weights[:, CACHE:].reshape(SPAN, N_SEQ, SPAN_DEV)
        cache_value_rows = value_head[:CACHE].astype(jnp.float32).reshape(N_SEQ, CACHE_DEV, HEAD_DIM)
        span_value_rows = value_head[CACHE:].astype(jnp.float32).reshape(N_SEQ, SPAN_DEV, HEAD_DIM)
        block_total_sum = jnp.einsum("lhy,hyg->lhg", cache_score_weights, cache_value_rows) + jnp.einsum("lhy,hyg->lhg", span_score_weights, span_value_rows)
        mass = jnp.sum(expo[:, :CACHE].reshape(SPAN, N_SEQ, CACHE_DEV), axis=2) + jnp.sum(expo[:, CACHE:].reshape(SPAN, N_SEQ, SPAN_DEV), axis=2)
        safe_mass = jnp.where(mass > 0.0, mass, 1.0)
        ratio = jnp.where(mass[..., None] > 0.0, block_total_sum / safe_mass[..., None], 0.0).astype(jnp.bfloat16)
        numerator = jnp.sum(mass[..., None] * ratio.astype(jnp.float32), axis=1)
        totals = jnp.sum(mass, axis=1)
        return (numerator / totals[:, None]).astype(jnp.bfloat16)

    per_head = lax.map(one_head, jnp.arange(HEADS, dtype=jnp.int32))
    return jnp.transpose(per_head, (1, 0, 2)).reshape(SPAN, HEADS * HEAD_DIM)
```

```python
import functools

import jax
import jax.numpy as jnp
from jax import lax
from jax.experimental import pallas as pl
from jax.experimental.pallas import tpu as pltpu
from jax.sharding import PartitionSpec as P

HEAD_DIM = 128
SCORE_SCALE = 168.0 ** (-0.5)
MASKED_SCORE = -1e30
PEAK_FLOOR = -1e29
MESH = pl.DeviceIdType.MESH

QRY, VALID, KEY, SPAN_KEY, VAL, SPAN_VAL = range(6)


def kernel(G, NP, q_ref, sk_ref, sv_ref, ck_ref, cv_ref, vld_ref, start_ref, out_ref,
           qa, kbuf, vbuf, skbuf, svbuf, vldbuf, bias, pc, ps, snum, sstat, rnum, rstat, fin,
           psend, precv, zsend, zrecv, fsend, frecv):
    me = lax.axis_index("seq")
    g = lax.rem(me, G)
    z = lax.div(me, G)
    S, C = sk_ref.shape[0], ck_ref.shape[0]
    QW = q_ref.shape[1] // G
    gs = QW // HEAD_DIM
    W = gs * G * S

    def member(d):
        return lax.rem(g + d, G)

    def plane(d):
        return lax.rem(z + d, NP)

    def cols(i, width):
        return pl.ds(pl.multiple_of(i * width, width), width)

    def source(kind, to):
        if kind == QRY:
            return q_ref.at[:, cols(to, QW)]
        if kind == VALID:
            return vld_ref
        ref = {KEY: ck_ref, SPAN_KEY: sk_ref, VAL: cv_ref, SPAN_VAL: sv_ref}[kind]
        return ref.at[:, cols(to, HEAD_DIM)]

    def landing(kind, frm):
        if kind == QRY:
            return qa.at[z, frm]
        return {VALID: vldbuf, KEY: kbuf, SPAN_KEY: skbuf, VAL: vbuf, SPAN_VAL: svbuf}[kind].at[frm]

    def own(kind):
        return pltpu.make_async_copy(source(kind, g), landing(kind, g), precv.at[kind, g])

    def exchange(kind, d, frm):
        to = member(d)
        return pltpu.make_async_remote_copy(
            src_ref=source(kind, to), dst_ref=landing(kind, frm),
            send_sem=psend.at[kind, d], recv_sem=precv.at[kind, frm],
            device_id={"seq": z * G + to}, device_id_type=MESH)

    def plane_send(kind):
        for d in range(1, G):
            exchange(kind, d, g).start()

    def plane_wait(kind):
        own(kind).wait()
        for d in range(1, G):
            exchange(kind, d, member(d)).wait_recv()

    def across(kind, d, src, dst, frm):
        return pltpu.make_async_remote_copy(
            src_ref=src, dst_ref=dst,
            send_sem=zsend.at[kind, d], recv_sem=zrecv.at[kind, frm],
            device_id={"seq": plane(d) * G + g}, device_id_type=MESH)

    def q_across(d, frm):
        return across(0, d, qa.at[z], qa.at[frm], frm)

    def num_across(d, frm):
        return across(1, d, snum.at[d], rnum.at[frm], frm)

    def stat_across(d, frm):
        return across(2, d, sstat.at[d], rstat.at[frm], frm)

    def result(d, frm):
        to = member(d)
        return pltpu.make_async_remote_copy(
            src_ref=fin.at[to], dst_ref=out_ref.at[:, cols(frm, QW)],
            send_sem=fsend.at[d], recv_sem=frecv.at[frm],
            device_id={"seq": z * G + to}, device_id_type=MESH)

    for kind in range(6):
        own(kind).start()
    barrier = pltpu.get_barrier_semaphore()
    for d in range(1, NP):
        pl.semaphore_signal(barrier, inc=1, device_id={"seq": plane(d) * G + g}, device_id_type=MESH)
    for d in range(1, G):
        pl.semaphore_signal(barrier, inc=1, device_id={"seq": z * G + member(d)}, device_id_type=MESH)
    pl.semaphore_wait(barrier, G - 1 + NP - 1)

    for kind in range(6):
        plane_send(kind)

    plane_wait(QRY)
    for d in range(1, NP):
        q_across(d, z).start()

    plane_wait(VALID)
    start = start_ref[0]
    lane = lax.broadcasted_iota(jnp.int32, (1, C), 1)
    for m in range(G):
        live = (vldbuf[m] == 1) & ((z * G + m) * C + lane < start)
        row = jnp.where(live, 0.0, MASKED_SCORE)
        bias[m] = jnp.transpose(jnp.broadcast_to(row, (128, C)))

    plane_wait(KEY)
    plane_wait(SPAN_KEY)
    nt = (((1,), (1,)), ((), ()))
    tn = (((0,), (0,)), ((), ()))
    keys = kbuf[...].reshape(G * C, HEAD_DIM)
    span_keys = skbuf[...].astype(jnp.float32).reshape(G * S, HEAD_DIM).astype(jnp.bfloat16)
    key_row = lax.broadcasted_iota(jnp.int32, (G * S, W), 0) + z * (G * S)
    query_col = lax.rem(lax.broadcasted_iota(jnp.int32, (G * S, W), 1), G * S)
    order = [0] + list(range(1, NP))
    for d in order:
        zp = plane(d)
        if d:
            q_across(d, zp).wait_recv()
        rows = qa[zp].astype(jnp.float32).reshape(G * S, QW).astype(jnp.bfloat16)
        qb = jnp.concatenate([rows[:, h * HEAD_DIM:(h + 1) * HEAD_DIM] for h in range(gs)], axis=0)
        s_c = lax.dot_general(keys, qb, nt, preferred_element_type=jnp.float32) * SCORE_SCALE
        s_c = s_c + bias[...].reshape(G * C, 128)[:, :W]
        s_s = lax.dot_general(span_keys, qb, nt, preferred_element_type=jnp.float32) * SCORE_SCALE
        s_s = jnp.where(key_row <= query_col + zp * (G * S), s_s, MASKED_SCORE)
        peak = jnp.maximum(jnp.max(s_c, axis=0, keepdims=True), jnp.max(s_s, axis=0, keepdims=True))
        peak = jnp.maximum(peak, PEAK_FLOOR)
        e_c = jnp.exp(s_c - peak)
        e_s = jnp.exp(s_s - peak)
        mass = jnp.sum(e_c, axis=0, keepdims=True) + jnp.sum(e_s, axis=0, keepdims=True)
        pc[d] = e_c.astype(jnp.bfloat16)
        ps[d] = e_s.astype(jnp.bfloat16)
        if d:
            sstat[d, 0:1] = peak
            sstat[d, 1:2] = mass
            stat_across(d, z).start()
        else:
            rstat[z, 0:1] = peak
            rstat[z, 1:2] = mass

    plane_wait(VAL)
    plane_wait(SPAN_VAL)
    vals = vbuf[...].reshape(G * C, HEAD_DIM)
    span_vals = svbuf[...].astype(jnp.float32).reshape(G * S, HEAD_DIM).astype(jnp.bfloat16)
    for d in list(range(NP - 1, 0, -1)) + [0]:
        num = lax.dot_general(vals, pc[d], tn, preferred_element_type=jnp.float32)
        num = num + lax.dot_general(span_vals, ps[d], tn, preferred_element_type=jnp.float32)
        if d:
            snum[d] = num.astype(jnp.bfloat16)
            num_across(d, z).start()
        else:
            rnum[z] = num.astype(jnp.bfloat16)

    for d in range(1, NP):
        stat_across(d, plane(d)).wait_recv()
    peaks = [rstat[p, 0:1] for p in range(NP)]
    top = functools.reduce(jnp.maximum, peaks)
    weights = [jnp.exp(peak - top) for peak in peaks]
    total = sum(weights[p] * rstat[p, 1:2] for p in range(NP))
    for d in range(1, NP):
        num_across(d, plane(d)).wait_recv()
    acc = sum(weights[p] * rnum[p].astype(jnp.float32) for p in range(NP))
    final = jnp.transpose(acc / total)
    for h in range(gs):
        piece = final[h * G * S:(h + 1) * G * S].reshape(G, S, HEAD_DIM)
        fin[:, :, h * HEAD_DIM:(h + 1) * HEAD_DIM] = piece.astype(jnp.bfloat16)
    for d in range(1, G):
        result(d, g).start()
    mine = pltpu.make_async_copy(fin.at[g], out_ref.at[:, cols(g, QW)], frecv.at[g])
    mine.start()

    for kind in range(6):
        for d in range(1, G):
            exchange(kind, d, g).wait_send()
    for d in range(1, NP):
        q_across(d, z).wait_send()
        stat_across(d, z).wait_send()
        num_across(d, z).wait_send()
    mine.wait()
    for d in range(1, G):
        result(d, member(d)).wait_recv()
    for d in range(1, G):
        result(d, g).wait_send()


def body(n_seq, queries, span_keys, span_values, cache_keys, cache_values, cache_valid, span_start):
    S, C = span_keys.shape[0], cache_keys.shape[0]
    G = span_keys.shape[1] // HEAD_DIM
    NP = n_seq // G
    QW = queries.shape[1] // G
    W = QW // HEAD_DIM * G * S
    bf16, f32 = jnp.bfloat16, jnp.float32
    hbm = pl.BlockSpec(memory_space=pl.ANY)
    return pl.pallas_call(
        functools.partial(kernel, G, NP),
        out_shape=jax.ShapeDtypeStruct(queries.shape, bf16),
        in_specs=[hbm] * 6 + [pl.BlockSpec(memory_space=pltpu.SMEM)],
        out_specs=pl.BlockSpec(memory_space=pltpu.VMEM),
        scratch_shapes=[
            pltpu.VMEM((NP, G, S, QW), bf16),
            pltpu.VMEM((G, C, HEAD_DIM), bf16),
            pltpu.VMEM((G, C, HEAD_DIM), bf16),
            pltpu.VMEM((G, S, HEAD_DIM), bf16),
            pltpu.VMEM((G, S, HEAD_DIM), bf16),
            pltpu.VMEM((G, 1, C), jnp.int32),
            pltpu.VMEM((G, C, 128), f32),
            pltpu.VMEM((NP, G * C, W), bf16),
            pltpu.VMEM((NP, G * S, W), bf16),
            pltpu.VMEM((NP, HEAD_DIM, W), bf16),
            pltpu.VMEM((NP, 2, W), f32),
            pltpu.VMEM((NP, HEAD_DIM, W), bf16),
            pltpu.VMEM((NP, 2, W), f32),
            pltpu.VMEM((G, S, QW), bf16),
            pltpu.SemaphoreType.DMA((6, G)),
            pltpu.SemaphoreType.DMA((6, G)),
            pltpu.SemaphoreType.DMA((3, NP)),
            pltpu.SemaphoreType.DMA((3, NP)),
            pltpu.SemaphoreType.DMA((G,)),
            pltpu.SemaphoreType.DMA((G,)),
        ],
        compiler_params=pltpu.CompilerParams(collective_id=0, has_side_effects=True),
    )(queries, span_keys, span_values, cache_keys, cache_values, cache_valid.reshape(1, C), span_start)


def solution(mesh):
    placed = (
        P(("groups", "seq"), "tensor"),
        P(("groups", "seq"), "tensor"),
        P(("groups", "seq"), "tensor"),
        P(("groups", "seq"), "tensor"),
        P(("groups", "seq"), "tensor"),
        P(("groups", "seq")),
        P("groups"),
    )
    return jax.shard_map(
        functools.partial(body, mesh.shape["seq"]), mesh=mesh, in_specs=placed,
        out_specs=P(("groups", "seq"), "tensor"), check_vma=False
    )
```

```python
import functools

import jax
import jax.numpy as jnp
from jax import lax
from jax.experimental import pallas as pl
from jax.experimental.pallas import tpu as pltpu
from jax.sharding import PartitionSpec as P

HEAD_DIM = 128
SCORE_SCALE = 168.0 ** (-0.5)
MASKED_SCORE = -1e30
PEAK_FLOOR = -1e29
MESH = pl.DeviceIdType.MESH

QRY, VALID, KEY, SPAN_KEY, VAL, SPAN_VAL = range(6)


def kernel(G, NP, q_ref, sk_ref, sv_ref, ck_ref, cv_ref, vld_ref, start_ref, out_ref,
           qa, kbuf, vbuf, skbuf, svbuf, vldbuf, bias, pc, ps, snum, sstat, rnum, rstat, mix, mix_t,
           psend, precv, zsend, zrecv, nsend, nrecv, ssend, srecv, ready):
    me = lax.axis_index("seq")
    g = lax.rem(me, G)
    z = lax.div(me, G)
    S, C = sk_ref.shape[0], ck_ref.shape[0]
    QW = q_ref.shape[1] // G
    gs = QW // HEAD_DIM
    W = gs * G * S

    def member(d):
        return lax.rem(g + d, G)

    def plane(d):
        return lax.rem(z + d, NP)

    def cols(i, width):
        return pl.ds(pl.multiple_of(i * width, width), width)

    def source(kind, to):
        if kind == QRY:
            return q_ref.at[:, cols(to, QW)]
        if kind == VALID:
            return vld_ref
        ref = {KEY: ck_ref, SPAN_KEY: sk_ref, VAL: cv_ref, SPAN_VAL: sv_ref}[kind]
        return ref.at[:, cols(to, HEAD_DIM)]

    def landing(kind, frm):
        if kind == QRY:
            return qa.at[z, frm]
        return {VALID: vldbuf, KEY: kbuf, SPAN_KEY: skbuf, VAL: vbuf, SPAN_VAL: svbuf}[kind].at[frm]

    def own(kind):
        return pltpu.make_async_copy(source(kind, g), landing(kind, g), precv.at[kind, g])

    def exchange(kind, d, frm):
        to = member(d)
        return pltpu.make_async_remote_copy(
            src_ref=source(kind, to), dst_ref=landing(kind, frm),
            send_sem=psend.at[kind, d], recv_sem=precv.at[kind, frm],
            device_id={"seq": z * G + to}, device_id_type=MESH)

    def plane_send(kind):
        for d in range(1, G):
            exchange(kind, d, g).start()

    def plane_wait(kind):
        own(kind).wait()
        for d in range(1, G):
            exchange(kind, d, member(d)).wait_recv()

    def q_across(d, frm):
        return pltpu.make_async_remote_copy(
            src_ref=qa.at[z], dst_ref=qa.at[frm],
            send_sem=zsend.at[d], recv_sem=zrecv.at[frm],
            device_id={"seq": plane(d) * G + g}, device_id_type=MESH)

    def num_to(d, e, from_plane, from_member):
        to = member(e)
        return pltpu.make_async_remote_copy(
            src_ref=snum.at[d, to], dst_ref=rnum.at[from_plane, from_member],
            send_sem=nsend.at[d, e], recv_sem=nrecv.at[from_plane, from_member],
            device_id={"seq": plane(d) * G + to}, device_id_type=MESH)

    def stat_to(d, e, from_plane, from_member):
        return pltpu.make_async_remote_copy(
            src_ref=sstat.at[d], dst_ref=rstat.at[from_plane, from_member],
            send_sem=ssend.at[d, e], recv_sem=srecv.at[from_plane, from_member],
            device_id={"seq": plane(d) * G + member(e)}, device_id_type=MESH)

    others = [(d, e) for d in range(NP - 1, -1, -1) for e in range(G) if d or e]

    for kind in range(6):
        own(kind).start()
    barrier = pltpu.get_barrier_semaphore()
    for d in range(1, NP):
        pl.semaphore_signal(barrier, inc=1, device_id={"seq": plane(d) * G + g}, device_id_type=MESH)
    for d in range(1, G):
        pl.semaphore_signal(barrier, inc=1, device_id={"seq": z * G + member(d)}, device_id_type=MESH)
    pl.semaphore_wait(barrier, G - 1 + NP - 1)

    for d in range(1, NP):
        pl.semaphore_signal(ready, inc=1, device_id={"seq": plane(d) * G + g}, device_id_type=MESH)
    for kind in range(6):
        plane_send(kind)

    plane_wait(QRY)
    for d in range(1, NP):
        q_across(d, z).start()

    plane_wait(VALID)
    start = start_ref[0]
    lane = lax.broadcasted_iota(jnp.int32, (1, C), 1)
    for m in range(G):
        live = (vldbuf[m] == 1) & ((z * G + m) * C + lane < start)
        row = jnp.where(live, 0.0, MASKED_SCORE)
        bias[m] = jnp.transpose(jnp.broadcast_to(row, (128, C)))

    pl.semaphore_wait(ready, NP - 1)
    plane_wait(KEY)
    plane_wait(SPAN_KEY)
    nt = (((1,), (1,)), ((), ()))
    tn = (((0,), (0,)), ((), ()))
    keys = kbuf[...].reshape(G * C, HEAD_DIM)
    span_keys = skbuf[...].astype(jnp.float32).reshape(G * S, HEAD_DIM).astype(jnp.bfloat16)
    key_row = lax.broadcasted_iota(jnp.int32, (G * S, W), 0) + z * (G * S)
    query_col = lax.rem(lax.broadcasted_iota(jnp.int32, (G * S, W), 1), G * S)
    order = [0] + list(range(1, NP))
    for d in order:
        zp = plane(d)
        if d:
            q_across(d, zp).wait_recv()
        rows = qa[zp].astype(jnp.float32).reshape(G * S, QW).astype(jnp.bfloat16)
        qb = jnp.concatenate([rows[:, h * HEAD_DIM:(h + 1) * HEAD_DIM] for h in range(gs)], axis=0)
        s_c = lax.dot_general(keys, qb, nt, preferred_element_type=jnp.float32) * SCORE_SCALE
        s_c = s_c + bias[...].reshape(G * C, 128)[:, :W]
        s_s = lax.dot_general(span_keys, qb, nt, preferred_element_type=jnp.float32) * SCORE_SCALE
        s_s = jnp.where(key_row <= query_col + zp * (G * S), s_s, MASKED_SCORE)
        peak = jnp.maximum(jnp.max(s_c, axis=0, keepdims=True), jnp.max(s_s, axis=0, keepdims=True))
        peak = jnp.maximum(peak, PEAK_FLOOR)
        e_c = jnp.exp(s_c - peak)
        e_s = jnp.exp(s_s - peak)
        mass = jnp.sum(e_c, axis=0, keepdims=True) + jnp.sum(e_s, axis=0, keepdims=True)
        pc[d] = e_c.astype(jnp.bfloat16)
        ps[d] = e_s.astype(jnp.bfloat16)
        sstat[d, 0:1] = peak
        sstat[d, 1:2] = mass
        if d == 0:
            rstat[z, g, 0:1] = peak
            rstat[z, g, 1:2] = mass
        for e in range(G):
            if d or e:
                stat_to(d, e, z, g).start()

    plane_wait(VAL)
    plane_wait(SPAN_VAL)
    vals = vbuf[...].reshape(G * C, HEAD_DIM)
    span_vals = svbuf[...].astype(jnp.float32).reshape(G * S, HEAD_DIM).astype(jnp.bfloat16)
    for d in list(range(NP - 1, 0, -1)) + [0]:
        num = lax.dot_general(vals, pc[d], tn, preferred_element_type=jnp.float32)
        num = num + lax.dot_general(span_vals, ps[d], tn, preferred_element_type=jnp.float32)
        rows = jnp.transpose(num)
        for h in range(gs):
            piece = rows[h * G * S:(h + 1) * G * S].reshape(G, S, HEAD_DIM)
            snum[d, :, :, h * HEAD_DIM:(h + 1) * HEAD_DIM] = piece.astype(jnp.bfloat16)
        for e in range(G):
            if d or e:
                num_to(d, e, z, g).start()
    rnum[z, g] = snum[0, g]

    for d, e in others:
        stat_to(d, e, plane(d), member(e)).wait_recv()
    peaks = [rstat[p, :, 0, :] for p in range(NP)]
    top = functools.reduce(jnp.maximum, peaks)
    weights = [jnp.exp(peak - top) for peak in peaks]
    total = sum(weights[p] * rstat[p, :, 1, :] for p in range(NP))
    mix[...] = jnp.zeros_like(mix)
    for p in range(NP):
        mix[p * G:(p + 1) * G, 0:W] = weights[p] / total
    mix_t[...] = jnp.transpose(mix[...])
    for kind in range(6):
        for d in range(1, G):
            exchange(kind, d, g).wait_send()
    for d in range(1, NP):
        q_across(d, z).wait_send()
    for d, e in others:
        stat_to(d, e, z, g).wait_send()
    for d, e in others:
        num_to(d, e, plane(d), member(e)).wait_recv()
    for h in range(gs):
        share = mix_t[pl.ds(pl.multiple_of(h * G * S + g * S, S), S), :]
        for m in range(G):
            acc = sum(
                share[:, p * G + m:p * G + m + 1]
                * rnum[p, m, :, h * HEAD_DIM:(h + 1) * HEAD_DIM].astype(jnp.float32)
                for p in range(NP))
            at = m * QW + h * HEAD_DIM
            out_ref[:, at:at + HEAD_DIM] = acc.astype(jnp.bfloat16)
    for d, e in others:
        num_to(d, e, z, g).wait_send()


def body(n_seq, queries, span_keys, span_values, cache_keys, cache_values, cache_valid, span_start):
    S, C = span_keys.shape[0], cache_keys.shape[0]
    G = span_keys.shape[1] // HEAD_DIM
    NP = n_seq // G
    QW = queries.shape[1] // G
    W = QW // HEAD_DIM * G * S
    bf16, f32 = jnp.bfloat16, jnp.float32
    hbm = pl.BlockSpec(memory_space=pl.ANY)
    return pl.pallas_call(
        functools.partial(kernel, G, NP),
        out_shape=jax.ShapeDtypeStruct(queries.shape, bf16),
        in_specs=[hbm] * 6 + [pl.BlockSpec(memory_space=pltpu.SMEM)],
        out_specs=pl.BlockSpec(memory_space=pltpu.VMEM),
        scratch_shapes=[
            pltpu.VMEM((NP, G, S, QW), bf16),
            pltpu.VMEM((G, C, HEAD_DIM), bf16),
            pltpu.VMEM((G, C, HEAD_DIM), bf16),
            pltpu.VMEM((G, S, HEAD_DIM), bf16),
            pltpu.VMEM((G, S, HEAD_DIM), bf16),
            pltpu.VMEM((G, 1, C), jnp.int32),
            pltpu.VMEM((G, C, 128), f32),
            pltpu.VMEM((NP, G * C, W), bf16),
            pltpu.VMEM((NP, G * S, W), bf16),
            pltpu.VMEM((NP, G, S, QW), bf16),
            pltpu.VMEM((NP, 2, W), f32),
            pltpu.VMEM((NP, G, S, QW), bf16),
            pltpu.VMEM((NP, G, 2, W), f32),
            pltpu.VMEM((128, 128), f32),
            pltpu.VMEM((128, 128), f32),
            pltpu.SemaphoreType.DMA((6, G)),
            pltpu.SemaphoreType.DMA((6, G)),
            pltpu.SemaphoreType.DMA((NP,)),
            pltpu.SemaphoreType.DMA((NP,)),
            pltpu.SemaphoreType.DMA((NP, G)),
            pltpu.SemaphoreType.DMA((NP, G)),
            pltpu.SemaphoreType.DMA((NP, G)),
            pltpu.SemaphoreType.DMA((NP, G)),
            pltpu.SemaphoreType.REGULAR,
        ],
        compiler_params=pltpu.CompilerParams(collective_id=0, has_side_effects=True),
    )(queries, span_keys, span_values, cache_keys, cache_values, cache_valid.reshape(1, C), span_start)


def solution(mesh):
    placed = (
        P(("groups", "seq"), "tensor"),
        P(("groups", "seq"), "tensor"),
        P(("groups", "seq"), "tensor"),
        P(("groups", "seq"), "tensor"),
        P(("groups", "seq"), "tensor"),
        P(("groups", "seq")),
        P("groups"),
    )
    return jax.shard_map(
        functools.partial(body, mesh.shape["seq"]), mesh=mesh, in_specs=placed,
        out_specs=P(("groups", "seq"), "tensor"), check_vma=False
    )
```
